32 devices in a mesh: grp: 4 (over z), fsdp: 8 (over y, x, core).
Axes of the slice: x: 2, y: 2, z: 4, core: 2. Of those that a mesh axis runs over, the one named last changes fastest.
Arguments:
- acts: bfloat16 [64, 128, 4096], P(('grp', 'fsdp'))
- out_grads: bfloat16 [64, 128, 1024], P(('grp', 'fsdp'))
- doc_lengths: int32 [64], P(('grp', 'fsdp')), may hold values from 32 to 128
- proj_in: bfloat16 [64, 4096], replicated, may hold values from -0.09375 to 0.09375
- proj_out: bfloat16 [64, 1024], replicated, may hold values from -0.1875 to 0.1875
- store_grads: bfloat16 [7168, 4096], P(('grp', 'fsdp')), may hold values from -6 to 6
- queries: bfloat16 [512, 4096], P('fsdp'), may hold values from -6 to 6
Outputs:
- new_grads: bfloat16 [64, 4096], P(('grp', 'fsdp'))
- store_scores: bfloat16 [7168, 512], P(('grp', 'fsdp'))
- new_scores: bfloat16 [64, 512], P(('grp', 'fsdp'))
The draws below stay inside these ranges and needn't reach their ends.
All inputs are finite; a program needn't handle non-finite values.
Results may differ from the reference program's by a relative error of at most 0.012.
The reference program's roundings to bfloat16 on the way (of `prepared`) count: a program that leaves them out, or rounds other values in their place, can miss the bound.
Values may be sent and summed in bfloat16 or wider, within the bound.
A program may use at most 64 MiB of HBM per device.

```python
import jax
import jax.numpy as jnp
from jax import lax

D = 4096
KV = 1024
R = 64
LEN = 128
QUERIES = 512
DOCS = 64
STORE = 7168


def document_scales(key):
    doc_index = jnp.arange(DOCS).astype(jnp.float32)
    rising = 1.0 + 2.0 * doc_index / max(DOCS - 1, 1)
    spread = jnp.exp(jax.random.uniform(key, (DOCS,), jnp.float32, -1.15, 1.15))
    return rising * spread


def token_field(key, features):
    keys = jax.random.split(key, 3)
    scales = document_scales(keys[0])
    noise = jax.random.normal(keys[1], (DOCS, LEN, features), jnp.float32)
    center = 0.7 * jax.random.normal(keys[2], (features,), jnp.float32)
    return scales[:, None, None] * (noise + center)


def draw_acts(key, part):
    return token_field(jax.random.fold_in(key, 101), D).astype(jnp.bfloat16)


def draw_out_grads(key, part):
    return token_field(jax.random.fold_in(key, 202), KV).astype(jnp.bfloat16)


def touch_ends(entries, stream_key, least, high):
    longest = entries.shape.index(max(entries.shape))
    spots = []
    for shift in (0, 1):
        where = [jax.random.randint(jax.random.fold_in(stream_key, axis), (), 0, length) for axis, length in enumerate(entries.shape)]
        where[longest] = (where[longest] + shift) % entries.shape[longest]
        spots.append(tuple(where))
    return entries.at[spots[0]].set(least).at[spots[1]].set(high)


def steps_of(stream_key, shape, cuts, low, high):
    loudness = 1.0
    for position, blocks in cuts:
        heights = jax.random.uniform(jax.random.fold_in(jax.random.fold_in(stream_key, 6), position), (blocks,), jnp.float32, low / len(cuts), high / len(cuts))
        loudness = loudness * jnp.repeat(jnp.exp(heights), shape[position] // blocks).reshape((-1,) + (1,) * (len(shape) - 1 - position))
    return loudness


def centred(rng, dims, width, limit, pieces=(), kind=jnp.bfloat16):
    array = jax.random.normal(rng, dims, jnp.float32) * width
    if len(pieces) > 0:
        array = steps_of(rng, dims, pieces, -0.22, 0.18) * array
    return jnp.clip(array, min=-limit, max=limit).astype(kind)


def setup_inputs(seed: int = 0) -> dict:
    splits = jax.random.split(jax.random.key(seed), 8)
    return {
        "acts": draw_acts(jax.random.fold_in(splits[7], 71), 0),
        "out_grads": draw_out_grads(jax.random.fold_in(splits[7], 71), 0),
        "doc_lengths": touch_ends(jax.random.randint(splits[2], (DOCS,), LEN // 4, LEN + 1), jax.random.fold_in(splits[2], 1), LEN // 4, LEN).astype(jnp.int32),
        "proj_in": centred(splits[3], (R, D), D ** -0.5, 0.09375),
        "proj_out": centred(splits[4], (R, KV), KV ** -0.5, 0.1875),
        "store_grads": centred(splits[5], (STORE, R * R), 1.0, 6.0, ((0, 32),)),
        "queries": centred(splits[6], (QUERIES, R * R), 1.0, 6.0, ((0, 8),)),
    }


def damped_inverse(summed, token_count, identity_matrix):
    covariance = summed / token_count
    damped = covariance + 0.1 * jnp.trace(covariance) / R * identity_matrix
    lower_factor = jnp.linalg.cholesky(damped)
    return jax.scipy.linalg.cho_solve((lower_factor, True), identity_matrix)

def precondition(query_rows, out_inverse, in_inverse):
    query_mats = query_rows.astype(jnp.float32).reshape(query_rows.shape[0], R, R)
    half_done = jnp.einsum('ab,qbc->qac', out_inverse, query_mats, precision=lax.Precision.HIGHEST)
    precond = jnp.einsum('qac,cd->qad', half_done, in_inverse, precision=lax.Precision.HIGHEST)
    return precond.reshape(query_rows.shape[0], R * R).astype(jnp.bfloat16)

def reference(acts, out_grads, doc_lengths, proj_in, proj_out, store_grads, queries):
    positions = lax.broadcasted_iota(jnp.int32, (DOCS, LEN), 1)
    valid_mask = (positions < doc_lengths[:, None]).astype(jnp.float32)
    in_proj = jnp.dot(acts.reshape(DOCS * LEN, D).astype(jnp.float32), proj_in.T.astype(jnp.float32), preferred_element_type=jnp.float32).reshape(DOCS, LEN, R)
    out_proj = jnp.dot(out_grads.reshape(DOCS * LEN, KV).astype(jnp.float32), proj_out.T.astype(jnp.float32), preferred_element_type=jnp.float32).reshape(DOCS, LEN, R)
    in_masked = in_proj * valid_mask[:, :, None]
    out_masked = out_proj * valid_mask[:, :, None]
    in_factor = jnp.einsum('dta,dtb->ab', in_masked, in_proj, precision=lax.Precision.HIGHEST)
    out_factor = jnp.einsum('dta,dtb->ab', out_masked, out_proj, precision=lax.Precision.HIGHEST)
    token_count = jnp.sum(valid_mask)
    per_doc = jnp.einsum('dta,dtb->dab', out_masked, in_proj, precision=lax.Precision.HIGHEST)
    per_doc = per_doc / doc_lengths.astype(jnp.float32)[:, None, None]
    new_grads = per_doc.reshape(DOCS, R * R).astype(jnp.bfloat16)
    identity_matrix = jnp.eye(R, dtype=jnp.float32)
    in_inverse = damped_inverse(in_factor, token_count, identity_matrix)
    out_inverse = damped_inverse(out_factor, token_count, identity_matrix)
    prepared = precondition(queries, out_inverse, in_inverse)
    store_scores = jnp.dot(store_grads.astype(jnp.float32), prepared.T.astype(jnp.float32), preferred_element_type=jnp.float32).astype(jnp.bfloat16)
    new_scores = jnp.dot(new_grads.astype(jnp.float32), prepared.T.astype(jnp.float32), preferred_element_type=jnp.float32).astype(jnp.bfloat16)
    return (new_grads, store_scores, new_scores)
```

```python
import functools

import jax
import jax.numpy as jnp
from jax import lax
from jax.experimental import pallas as pl
from jax.experimental.pallas import tpu as pltpu
from jax.sharding import PartitionSpec as P

F32 = jnp.float32
BF16 = jnp.bfloat16
ANY = pl.ANY
VMEM = pltpu.VMEM
HIGHEST = lax.Precision.HIGHEST
NT = (((1,), (1,)), ((), ()))
TN = (((0,), (0,)), ((), ()))


def invert_pair(matrix, rank):
    rows = lax.broadcasted_iota(jnp.int32, matrix.shape, 0)
    lanes = lax.broadcasted_iota(jnp.int32, matrix.shape, 1)
    left = lanes < rank
    local = jnp.where(left, lanes, lanes - rank)
    for k in range(rank):
        column = jnp.where(left, matrix[:, k : k + 1], matrix[:, rank + k : rank + k + 1])
        inverse_pivot = 1.0 / column[k : k + 1, :]
        at_pivot = local == k
        scaled = jnp.where(at_pivot[k : k + 1, :], 1.0, matrix[k : k + 1, :]) * inverse_pivot
        reduced = jnp.where(at_pivot, 0.0, matrix) - column * scaled
        matrix = jnp.where(rows == k, scaled, reduced)
    return matrix


def collect_kernel(
    n_grp, n_fsdp,
    lengths, acts, out_grads, proj_in, proj_out, queries,
    inverses, new_grads, gathered,
    acts_v, outg_v, pin_v, pout_v, plane_slots, column_slots, partial,
    load_sems, own_sem, gs, gr, fs, fr, ps, pr, cs, cr,
):
    g = lax.axis_index("grp")
    f = lax.axis_index("fsdp")
    n_docs, length, features = acts.shape
    rank = proj_in.shape[0]
    here = queries.shape[0]
    half = n_fsdp // 2
    partner = f + 1 - 2 * lax.rem(f, 2)

    loads = [
        pltpu.make_async_copy(src, dst, load_sems.at[i])
        for i, (src, dst) in enumerate(
            ((acts, acts_v), (proj_in, pin_v), (out_grads, outg_v), (proj_out, pout_v))
        )
    ]
    for load in loads:
        load.start()

    barrier = pltpu.get_barrier_semaphore()

    def greet_plane(d, _):
        pl.semaphore_signal(barrier, inc=1, device_id={"grp": g, "fsdp": lax.rem(f + d, n_fsdp)},
                            device_id_type=pl.DeviceIdType.MESH)
        return 0

    def greet_column(d, _):
        pl.semaphore_signal(barrier, inc=1, device_id={"grp": lax.rem(g + d, n_grp), "fsdp": f},
                            device_id_type=pl.DeviceIdType.MESH)
        return 0

    lax.fori_loop(1, n_fsdp, greet_plane, 0)
    lax.fori_loop(1, n_grp, greet_column, 0)
    pl.semaphore_wait(barrier, n_fsdp - 1 + n_grp - 1)

    def slot(index):
        return gathered.at[pl.ds(pl.multiple_of(index * here, here), here)]

    def shard_copy(d):
        return pltpu.make_async_remote_copy(
            src_ref=queries, dst_ref=slot(f), send_sem=gs.at[d], recv_sem=gr.at[d],
            device_id={"grp": g, "fsdp": lax.rem(f + 2 * d, n_fsdp)},
            device_id_type=pl.DeviceIdType.MESH)

    def pass_copy(d):
        source = lax.rem(f + n_fsdp - 2 * d, n_fsdp)
        return pltpu.make_async_remote_copy(
            src_ref=queries if d == 0 else slot(source), dst_ref=slot(f if d == 0 else source),
            send_sem=fs.at[d], recv_sem=fr.at[d],
            device_id={"grp": g, "fsdp": partner},
            device_id_type=pl.DeviceIdType.MESH)

    for d in range(1, half):
        shard_copy(d).start()
    pass_copy(0).start()
    own = pltpu.make_async_copy(queries, slot(f), own_sem)
    own.start()

    for load in loads:
        load.wait()
    tokens = lax.broadcasted_iota(jnp.int32, (length, 2 * rank), 0)
    lanes = lax.broadcasted_iota(jnp.int32, (rank, 2 * rank), 1)
    rows = lax.broadcasted_iota(jnp.int32, (rank, 2 * rank), 0)
    total = jnp.zeros((2 * rank, 2 * rank), F32)
    count = 0
    for doc in range(n_docs):
        in_proj = lax.dot_general(acts_v[doc], pin_v[...], NT, preferred_element_type=F32)
        out_proj = lax.dot_general(outg_v[doc], pout_v[...], NT, preferred_element_type=F32)
        both = jnp.concatenate([in_proj, out_proj], axis=1)
        size = lengths[doc]
        both = jnp.where(tokens < size, both, 0.0)
        gram = lax.dot_general(both, both, TN, precision=HIGHEST, preferred_element_type=F32)
        total = total + gram
        count = count + jnp.minimum(size, length)
        new_grads[doc] = (gram[rank:, :rank] / size.astype(F32)).astype(BF16)
    partial[0:rank, :] = jnp.where(lanes < rank, total[:rank, :], total[rank:, :])
    partial[rank:, :] = jnp.zeros((8, 2 * rank), F32) + count.astype(F32)

    def plane_copy(d):
        return pltpu.make_async_remote_copy(
            src_ref=partial, dst_ref=plane_slots.at[f], send_sem=ps.at[d], recv_sem=pr.at[d],
            device_id={"grp": g, "fsdp": lax.rem(f + d, n_fsdp)},
            device_id_type=pl.DeviceIdType.MESH)

    for d in range(1, n_fsdp):
        plane_copy(d).start()
    plane_slots[f] = partial[...]
    for d in range(1, n_fsdp):
        plane_copy(d).wait()
    summed = plane_slots[0]
    for i in range(1, n_fsdp):
        summed = summed + plane_slots[i]
    column_slots[g] = summed

    def column_copy(d):
        return pltpu.make_async_remote_copy(
            src_ref=column_slots.at[g], dst_ref=column_slots.at[g], send_sem=cs.at[d], recv_sem=cr.at[d],
            device_id={"grp": lax.rem(g + d, n_grp), "fsdp": f},
            device_id_type=pl.DeviceIdType.MESH)

    for d in range(1, n_grp):
        column_copy(d).start()
    for d in range(1, n_grp):
        column_copy(d).wait()
    summed = column_slots[0]
    for i in range(1, n_grp):
        summed = summed + column_slots[i]

    covariance = summed[:rank, :] / summed[rank : rank + 1, :]
    diagonal = (rows == lanes) | (rows + rank == lanes)
    on_diagonal = jnp.where(diagonal, covariance, 0.0)
    in_trace = jnp.sum(jnp.where(lanes < rank, on_diagonal, 0.0))
    out_trace = jnp.sum(jnp.where(lanes < rank, 0.0, on_diagonal))
    ridge = jnp.where(lanes < rank, 0.1 * in_trace / rank, 0.1 * out_trace / rank)
    inverses[...] = invert_pair(covariance + jnp.where(diagonal, ridge, 0.0), rank)

    own.wait()
    for d in range(1, half):
        shard_copy(d).wait()
        pass_copy(d).start()
    for d in range(half):
        pass_copy(d).wait()


def collect(n_grp, n_fsdp, doc_lengths, acts, out_grads, proj_in, proj_out, queries):
    n_docs, length, _ = acts.shape
    rank = proj_in.shape[0]
    here, width = queries.shape
    dma = pltpu.SemaphoreType.DMA
    return pl.pallas_call(
        functools.partial(collect_kernel, n_grp, n_fsdp),
        out_shape=(
            jax.ShapeDtypeStruct((rank, 2 * rank), F32),
            jax.ShapeDtypeStruct((n_docs, rank, rank), BF16),
            jax.ShapeDtypeStruct((n_fsdp * here, width), BF16),
        ),
        in_specs=[pl.BlockSpec(memory_space=pltpu.SMEM)] + [pl.BlockSpec(memory_space=ANY)] * 5,
        out_specs=(
            pl.BlockSpec(memory_space=VMEM),
            pl.BlockSpec(memory_space=VMEM),
            pl.BlockSpec(memory_space=ANY),
        ),
        scratch_shapes=[
            VMEM(acts.shape, BF16), VMEM(out_grads.shape, BF16),
            VMEM(proj_in.shape, BF16), VMEM(proj_out.shape, BF16),
            VMEM((n_fsdp, rank + 8, 2 * rank), F32), VMEM((n_grp, rank + 8, 2 * rank), F32),
            VMEM((rank + 8, 2 * rank), F32),
            dma((4,)), dma,
            dma((n_fsdp // 2,)), dma((n_fsdp // 2,)), dma((n_fsdp // 2,)), dma((n_fsdp // 2,)),
            dma((n_fsdp,)), dma((n_fsdp,)), dma((n_grp,)), dma((n_grp,)),
        ],
        compiler_params=pltpu.CompilerParams(
            collective_id=0, has_side_effects=True, vmem_limit_bytes=24 * 2**20),
    )(doc_lengths, acts, out_grads, proj_in, proj_out, queries)


def split3(value):
    high = value.astype(BF16)
    rest = value - high.astype(F32)
    middle = rest.astype(BF16)
    low = (rest - middle.astype(F32)).astype(BF16)
    return high, middle, low


def score_kernel(inverses, new_grads, queries, store, store_out, new_out, work, score_rows, sem):
    stored, width = store.shape
    fresh = new_grads.shape[0]
    rank = inverses.shape[0]
    rows_padded = score_rows.shape[0]
    load = pltpu.make_async_copy(store, score_rows.at[pl.ds(0, stored)], sem)
    load.start()
    pad = rows_padded - stored
    score_rows[stored:, :] = jnp.concatenate(
        [new_grads[...].astype(F32), jnp.zeros((pad - fresh, width), F32)], axis=0).astype(BF16)

    block = 4 * rank
    groups = work.shape[0]
    both = inverses[...]
    in_inverse = both[:, :rank]
    out_inverse = both[:, rank:]
    wide = jnp.concatenate([in_inverse] * 4, axis=1)
    tiled = jnp.concatenate([wide] * 4, axis=0)
    r = lax.broadcasted_iota(jnp.int32, (block, block), 0) // rank
    c = lax.broadcasted_iota(jnp.int32, (block, block), 1) // rank
    pieces = split3(jnp.where(r == c, tiled, 0.0))
    for i in range(width // block):
        chunk = queries[:, i * block : (i + 1) * block]
        part = lax.dot_general(pieces[0], chunk, NT, preferred_element_type=F32)
        part = part + lax.dot_general(pieces[1], chunk, NT, preferred_element_type=F32)
        part = part + lax.dot_general(pieces[2], chunk, NT, preferred_element_type=F32)
        for j in range(groups):
            work[j, i * block : (i + 1) * block, :] = part[:, j * 128 : (j + 1) * 128]

    oh, om, ol = split3(out_inverse)
    left = jnp.concatenate([oh, oh, om, om, oh, ol], axis=1)

    def one(b, _):
        where = pl.ds(b, rank, stride=rank)
        half_done = jnp.concatenate([work[j, where, :] for j in range(groups)], axis=1)
        xh, xm, xl = split3(half_done)
        right = jnp.concatenate([xh, xm, xh, xm, xl, xh], axis=0)
        done = jnp.dot(left, right, preferred_element_type=F32)
        for j in range(groups):
            work[j, where, :] = done[:, j * 128 : (j + 1) * 128]
        return 0

    lax.fori_loop(0, rank, one, 0, unroll=4)
    load.wait()
    prepared = jnp.concatenate([work[j].astype(BF16) for j in range(groups)], axis=1)
    scores = jnp.dot(score_rows[...], prepared, preferred_element_type=F32)
    store_out[...] = scores[:stored].astype(BF16)
    new_out[...] = scores[stored : stored + fresh].astype(BF16)


def score(inverses, new_grads, gathered, store_grads):
    stored, width = store_grads.shape
    fresh = new_grads.shape[0]
    n_queries = gathered.shape[0]
    rows_padded = (stored + fresh + 15) // 16 * 16
    return pl.pallas_call(
        score_kernel,
        out_shape=(
            jax.ShapeDtypeStruct((stored, n_queries), BF16),
            jax.ShapeDtypeStruct((fresh, n_queries), BF16),
        ),
        in_specs=[pl.BlockSpec(memory_space=VMEM)] * 3 + [pl.BlockSpec(memory_space=ANY)],
        out_specs=(pl.BlockSpec(memory_space=VMEM), pl.BlockSpec(memory_space=VMEM)),
        scratch_shapes=[
            VMEM((n_queries // 128, width, 128), F32), VMEM((rows_padded, width), BF16),
            pltpu.SemaphoreType.DMA,
        ],
        compiler_params=pltpu.CompilerParams(vmem_limit_bytes=48 * 2**20),
    )(inverses, new_grads, gathered, store_grads)


def solution(mesh):
    n_grp, n_fsdp = mesh.shape["grp"], mesh.shape["fsdp"]

    def shards(acts, out_grads, doc_lengths, proj_in, proj_out, store_grads, queries):
        inverses, per_doc, gathered = collect(
            n_grp, n_fsdp, doc_lengths, acts, out_grads, proj_in, proj_out, queries)
        new_grads = per_doc.reshape(per_doc.shape[0], -1)
        store_scores, new_scores = score(inverses, new_grads, gathered, store_grads)
        return new_grads, store_scores, new_scores

    rows = P(("grp", "fsdp"), None)
    placed = (
        P(("grp", "fsdp"), None, None),
        P(("grp", "fsdp"), None, None),
        P(("grp", "fsdp")),
        P(),
        P(),
        rows,
        P("fsdp", None),
    )
    return jax.shard_map(
        shards, mesh=mesh, in_specs=placed, out_specs=(rows, rows, rows), check_vma=False)
```

```python
import functools

import jax
import jax.numpy as jnp
from jax import lax
from jax.experimental import pallas as pl
from jax.experimental.pallas import tpu as pltpu
from jax.sharding import PartitionSpec as P

F32 = jnp.float32
BF16 = jnp.bfloat16
ANY = pl.ANY
VMEM = pltpu.VMEM
HIGHEST = lax.Precision.HIGHEST
NT = (((1,), (1,)), ((), ()))
TN = (((0,), (0,)), ((), ()))


def invert_pair(matrix, rank):
    rows = lax.broadcasted_iota(jnp.int32, matrix.shape, 0)
    lanes = lax.broadcasted_iota(jnp.int32, matrix.shape, 1)
    left = lanes < rank
    local = jnp.where(left, lanes, lanes - rank)
    for k in range(rank):
        column = jnp.where(left, matrix[:, k : k + 1], matrix[:, rank + k : rank + k + 1])
        inverse_pivot = 1.0 / column[k : k + 1, :]
        at_pivot = local == k
        scaled = jnp.where(at_pivot[k : k + 1, :], 1.0, matrix[k : k + 1, :]) * inverse_pivot
        reduced = jnp.where(at_pivot, 0.0, matrix) - column * scaled
        matrix = jnp.where(rows == k, scaled, reduced)
    return matrix


def split3(value):
    high = value.astype(BF16)
    rest = value - high.astype(F32)
    middle = rest.astype(BF16)
    low = (rest - middle.astype(F32)).astype(BF16)
    return high, middle, low


def influence_kernel(
    n_grp, n_fsdp, early,
    lengths, acts, out_grads, proj_in, proj_out, queries, store,
    new_grads, store_out, new_out,
    acts_v, outg_v, pin_v, pout_v, gathered, score_rows, work, pieces, plane_slots, column_slots, totals,
    load_sems, gs, gr, fs, fr, ps, pr, cs, cr, ts, tr,
):
    g = lax.axis_index("grp")
    f = lax.axis_index("fsdp")
    n_docs, length, features = acts.shape
    rank = proj_in.shape[0]
    here, width = queries.shape
    stored = store.shape[0]
    half = n_fsdp // 2
    chip = f // 2
    core = lax.rem(f, 2)
    cut = here // PIECE
    share = rank // n_fsdp
    pitch = rank + 8
    mesh_id = pl.DeviceIdType.MESH

    def in_plane(d):
        return {"grp": g, "fsdp": lax.rem(f + d, n_fsdp)}

    def in_column(d):
        return {"grp": lax.rem(g + d, n_grp), "fsdp": f}

    def rows_of(index, p):
        return gathered.at[pl.ds(pl.multiple_of(index * here + p * PIECE, PIECE), PIECE)]

    def shard_copy(d, p):
        return pltpu.make_async_remote_copy(
            src_ref=queries.at[pl.ds(p * PIECE, PIECE)], dst_ref=rows_of(f, p),
            send_sem=gs.at[d * cut + p], recv_sem=gr.at[d * cut + p],
            device_id=in_plane(2 * d), device_id_type=mesh_id)

    def pass_copy(d, p):
        source = lax.rem(chip + half - d, half) * 2 + core
        return pltpu.make_async_remote_copy(
            src_ref=rows_of(source, p), dst_ref=rows_of(source, p),
            send_sem=fs.at[d * cut + p], recv_sem=fr.at[d * cut + p],
            device_id={"grp": g, "fsdp": f + 1 - 2 * core}, device_id_type=mesh_id)

    own_rows = gathered.at[pl.ds(pl.multiple_of(f * here, here), here)]
    loads = [
        pltpu.make_async_copy(src, dst, load_sems.at[i])
        for i, (src, dst) in enumerate((
            (acts, acts_v), (proj_in, pin_v), (out_grads, outg_v), (proj_out, pout_v),
            (queries, own_rows), (store, score_rows.at[pl.ds(0, stored)])))
    ]
    for load in loads:
        load.start()

    barrier = pltpu.get_barrier_semaphore()

    def greet_plane(d, _):
        pl.semaphore_signal(barrier, inc=1, device_id=in_plane(d), device_id_type=mesh_id)
        return 0

    def greet_column(d, _):
        pl.semaphore_signal(barrier, inc=1, device_id=in_column(d), device_id_type=mesh_id)
        return 0

    lax.fori_loop(1, n_fsdp, greet_plane, 0)
    lax.fori_loop(1, n_grp, greet_column, 0)
    pl.semaphore_wait(barrier, n_fsdp - 1 + n_grp - 1)

    for p in range(min(early, cut)):
        for d in range(1, half):
            shard_copy(d, p).start()
    for load in loads[:5]:
        load.wait()
    for p in range(cut):
        pass_copy(0, p).start()

    tokens = lax.broadcasted_iota(jnp.int32, (length, 2 * rank), 0)
    lanes = lax.broadcasted_iota(jnp.int32, (rank, 2 * rank), 1)
    rows = lax.broadcasted_iota(jnp.int32, (rank, 2 * rank), 0)
    total = jnp.zeros((2 * rank, 2 * rank), F32)
    count = 0
    per_doc = []
    for doc in range(n_docs):
        in_proj = lax.dot_general(acts_v[doc], pin_v[...], NT, preferred_element_type=F32)
        out_proj = lax.dot_general(outg_v[doc], pout_v[...], NT, preferred_element_type=F32)
        both = jnp.concatenate([in_proj, out_proj], axis=1)
        size = lengths[doc]
        both = jnp.where(tokens < size, both, 0.0)
        gram = lax.dot_general(both, both, TN, precision=HIGHEST, preferred_element_type=F32)
        total = total + gram
        count = count + jnp.minimum(size, length)
        per_doc.append(gram[rank:, :rank] / size.astype(F32))
    packed = jnp.where(lanes < rank, total[:rank, :], total[rank:, :])
    counts = jnp.zeros((8, 2 * rank), F32) + count.astype(F32)
    for i in range(n_fsdp):
        piece = packed[i * share : (i + 1) * share, :]
        if share < 8:
            piece = jnp.concatenate([piece, jnp.zeros((8 - share, 2 * rank), F32)], axis=0)
        pieces[i, : piece.shape[0], :] = piece
        pieces[i, piece.shape[0] :, :] = counts

    def scatter_copy(d):
        return pltpu.make_async_remote_copy(
            src_ref=pieces.at[lax.rem(f + d, n_fsdp)], dst_ref=plane_slots.at[f],
            send_sem=ps.at[d], recv_sem=pr.at[d], device_id=in_plane(d), device_id_type=mesh_id)

    def column_copy(d):
        return pltpu.make_async_remote_copy(
            src_ref=column_slots.at[g], dst_ref=column_slots.at[g],
            send_sem=cs.at[d], recv_sem=cr.at[d], device_id=in_column(d), device_id_type=mesh_id)

    def total_copy(d):
        return pltpu.make_async_remote_copy(
            src_ref=totals.at[f], dst_ref=totals.at[f],
            send_sem=ts.at[d], recv_sem=tr.at[d], device_id=in_plane(d), device_id_type=mesh_id)

    for d in range(1, n_fsdp):
        scatter_copy(d).start()
    plane_slots[f] = pieces[f]
    flat = [
        jnp.concatenate([grad[a : a + 1, :] for a in range(rank)], axis=1) for grad in per_doc
    ]
    fresh = jnp.concatenate(
        flat + [jnp.zeros((score_rows.shape[0] - stored - n_docs, width), F32)], axis=0).astype(BF16)
    score_rows[stored:, :] = fresh
    new_grads[...] = fresh[:n_docs]
    for d in range(1, n_fsdp):
        scatter_copy(d).wait()
    summed = plane_slots[0]
    for i in range(1, n_fsdp):
        summed = summed + plane_slots[i]
    column_slots[g] = summed
    for d in range(1, n_grp):
        column_copy(d).start()
    for d in range(1, n_grp):
        column_copy(d).wait()
    summed = column_slots[0]
    for i in range(1, n_grp):
        summed = summed + column_slots[i]
    totals[f] = summed
    for d in range(1, n_fsdp):
        total_copy(d).start()
    for p in range(min(early, cut), cut):
        for d in range(1, half):
            shard_copy(d, p).start()
    for d in range(1, n_fsdp):
        total_copy(d).wait()

    covariance = jnp.concatenate([totals[i, :share, :] for i in range(n_fsdp)], axis=0)
    covariance = covariance / summed[summed.shape[0] - 1 :, :]
    diagonal = (rows == lanes) | (rows + rank == lanes)
    on_diagonal = jnp.where(diagonal, covariance, 0.0)
    in_trace = jnp.sum(jnp.where(lanes < rank, on_diagonal, 0.0))
    out_trace = jnp.sum(jnp.where(lanes < rank, 0.0, on_diagonal))
    ridge = jnp.where(lanes < rank, 0.1 * in_trace / rank, 0.1 * out_trace / rank)
    both = invert_pair(covariance + jnp.where(diagonal, ridge, 0.0), rank)

    block = 4 * rank
    wide = jnp.concatenate([both[:, :rank]] * 4, axis=1)
    tiled = jnp.concatenate([wide] * 4, axis=0)
    r = lax.broadcasted_iota(jnp.int32, (block, block), 0) // rank
    c = lax.broadcasted_iota(jnp.int32, (block, block), 1) // rank
    in_parts = split3(jnp.where(r == c, tiled, 0.0))
    oh, om, ol = split3(both[:, rank:])
    left = jnp.concatenate([oh, oh, om, om, oh, ol], axis=1)

    load = loads[5]
    load.wait()
    unit_chips = UNIT // (2 * here)
    n_units = half // unit_chips

    def one_unit(e, _):
        unit = lax.rem(chip // unit_chips + n_units - e, n_units)
        for i in range(unit_chips):
            d = lax.rem(chip - (unit * unit_chips + i) + half, half)

            @pl.when(d != 0)
            def _():
                for p in range(cut):
                    shard_copy(d, p).wait()
                    pass_copy(d, p).start()

        for i in range(unit_chips):
            d = lax.rem(chip - (unit * unit_chips + i) + half, half)
            for p in range(cut):
                pass_copy(d, p).wait()
        here_rows = pl.ds(pl.multiple_of(unit * UNIT, UNIT), UNIT)
        for i in range(width // block):
            chunk = gathered[here_rows, i * block : (i + 1) * block]
            part = lax.dot_general(in_parts[0], chunk, NT, preferred_element_type=F32)
            part = part + lax.dot_general(in_parts[1], chunk, NT, preferred_element_type=F32)
            part = part + lax.dot_general(in_parts[2], chunk, NT, preferred_element_type=F32)
            for a in range(4):
                start = (4 * i + a) * pitch
                work[start : start + rank, :] = part[a * rank : (a + 1) * rank, :]
        for b in range(0, rank, 4):
            wheres = [pl.ds(b + j, rank, stride=pitch) for j in range(4)]
            half_done = jnp.concatenate([work[w, :] for w in wheres], axis=1)
            xh, xm, xl = split3(half_done)
            right = jnp.concatenate([xh, xm, xh, xm, xl, xh], axis=0)
            done = jnp.dot(left, right, preferred_element_type=F32)
            for j in range(4):
                work[wheres[j], :] = done[:, j * UNIT : (j + 1) * UNIT]
        prepared = jnp.concatenate(
            [work[a * pitch : a * pitch + rank, :].astype(BF16) for a in range(rank)], axis=0)
        scores = jnp.dot(score_rows[...], prepared, preferred_element_type=F32).astype(BF16)
        store_out[:, here_rows] = scores[:stored]
        new_out[:, here_rows] = scores[stored : stored + n_docs]
        return 0

    lax.fori_loop(0, n_units, one_unit, 0)


PIECE = 16
UNIT = 128


def influence(n_grp, n_fsdp, early, doc_lengths, acts, out_grads, proj_in, proj_out, queries, store):
    n_docs = acts.shape[0]
    rank = proj_in.shape[0]
    here, width = queries.shape
    stored = store.shape[0]
    n_queries = n_fsdp * here
    dma = pltpu.SemaphoreType.DMA
    slot = (-(-(rank // n_fsdp) // 8) * 8 + 8, 2 * rank)
    score_rows = -(-(stored + n_docs) // 16) * 16
    copies = dma((n_fsdp // 2 * (here // PIECE),))
    return pl.pallas_call(
        functools.partial(influence_kernel, n_grp, n_fsdp, early),
        out_shape=(
            jax.ShapeDtypeStruct((n_docs, width), BF16),
            jax.ShapeDtypeStruct((stored, n_queries), BF16),
            jax.ShapeDtypeStruct((n_docs, n_queries), BF16),
        ),
        in_specs=[pl.BlockSpec(memory_space=pltpu.SMEM)] + [pl.BlockSpec(memory_space=ANY)] * 6,
        out_specs=tuple([pl.BlockSpec(memory_space=VMEM)] * 3),
        scratch_shapes=[
            VMEM(acts.shape, BF16), VMEM(out_grads.shape, BF16),
            VMEM(proj_in.shape, BF16), VMEM(proj_out.shape, BF16),
            VMEM((n_queries, width), BF16), VMEM((score_rows, width), BF16),
            VMEM((rank * (rank + 8), UNIT), F32),
            VMEM((n_fsdp,) + slot, F32), VMEM((n_fsdp,) + slot, F32),
            VMEM((n_grp,) + slot, F32), VMEM((n_fsdp,) + slot, F32),
            dma((6,)), copies, copies, copies, copies,
            dma((n_fsdp,)), dma((n_fsdp,)), dma((n_grp,)), dma((n_grp,)), dma((n_fsdp,)), dma((n_fsdp,)),
        ],
        compiler_params=pltpu.CompilerParams(
            collective_id=0, has_side_effects=True, vmem_limit_bytes=60 * 2**20),
    )(doc_lengths, acts, out_grads, proj_in, proj_out, queries, store)


def solution(mesh):
    n_grp, n_fsdp = mesh.shape["grp"], mesh.shape["fsdp"]

    def shards(acts, out_grads, doc_lengths, proj_in, proj_out, store_grads, queries):
        return influence(
            n_grp, n_fsdp, 1, doc_lengths, acts, out_grads, proj_in, proj_out, queries, store_grads)

    rows = P(("grp", "fsdp"), None)
    placed = (
        P(("grp", "fsdp"), None, None),
        P(("grp", "fsdp"), None, None),
        P(("grp", "fsdp")),
        P(),
        P(),
        rows,
        P("fsdp", None),
    )
    return jax.shard_map(
        shards, mesh=mesh, in_specs=placed, out_specs=(rows, rows, rows), check_vma=False)
```

```python
import functools

import jax
import jax.numpy as jnp
from jax import lax
from jax.experimental import pallas as pl
from jax.experimental.pallas import tpu as pltpu
from jax.sharding import PartitionSpec as P

F32 = jnp.float32
BF16 = jnp.bfloat16
ANY = pl.ANY
VMEM = pltpu.VMEM
HIGHEST = lax.Precision.HIGHEST
NT = (((1,), (1,)), ((), ()))
TN = (((0,), (0,)), ((), ()))


def invert_pair(matrix, rank):
    rows = lax.broadcasted_iota(jnp.int32, matrix.shape, 0)
    lanes = lax.broadcasted_iota(jnp.int32, matrix.shape, 1)
    left = lanes < rank
    local = jnp.where(left, lanes, lanes - rank)
    for k in range(rank):
        column = jnp.where(left, matrix[:, k : k + 1], matrix[:, rank + k : rank + k + 1])
        inverse_pivot = 1.0 / column[k : k + 1, :]
        at_pivot = local == k
        scaled = jnp.where(at_pivot[k : k + 1, :], 1.0, matrix[k : k + 1, :]) * inverse_pivot
        reduced = jnp.where(at_pivot, 0.0, matrix) - column * scaled
        matrix = jnp.where(rows == k, scaled, reduced)
    return matrix


def split3(value):
    high = value.astype(BF16)
    rest = value - high.astype(F32)
    middle = rest.astype(BF16)
    low = (rest - middle.astype(F32)).astype(BF16)
    return high, middle, low


def influence_kernel(
    n_grp, n_fsdp, early,
    lengths, acts, out_grads, proj_in, proj_out, queries, store,
    new_grads, store_out, new_out,
    acts_v, outg_v, pin_v, pout_v, gathered, score_rows, work, pieces, plane_slots, column_slots, totals,
    load_sems, gs, gr, fs, fr, ps, pr, cs, cr, ts, tr,
):
    g = lax.axis_index("grp")
    f = lax.axis_index("fsdp")
    n_docs, length, features = acts.shape
    rank = proj_in.shape[0]
    here, width = queries.shape
    stored = store.shape[0]
    half = n_fsdp // 2
    chip = f // 2
    core = lax.rem(f, 2)
    cut = here // PIECE
    share = rank // n_fsdp
    pitch = rank + 8
    mesh_id = pl.DeviceIdType.MESH

    def in_plane(d):
        return {"grp": g, "fsdp": lax.rem(f + d, n_fsdp)}

    def in_column(d):
        return {"grp": lax.rem(g + d, n_grp), "fsdp": f}

    def rows_of(index, p):
        return gathered.at[pl.ds(pl.multiple_of(index * here + p * PIECE, PIECE), PIECE)]

    def shard_copy(d, p):
        return pltpu.make_async_remote_copy(
            src_ref=queries.at[pl.ds(p * PIECE, PIECE)], dst_ref=rows_of(f, p),
            send_sem=gs.at[d * cut + p], recv_sem=gr.at[d * cut + p],
            device_id=in_plane(2 * d), device_id_type=mesh_id)

    def pass_copy(d, p):
        source = lax.rem(chip + half - d, half) * 2 + core
        return pltpu.make_async_remote_copy(
            src_ref=rows_of(source, p), dst_ref=rows_of(source, p),
            send_sem=fs.at[d * cut + p], recv_sem=fr.at[d * cut + p],
            device_id={"grp": g, "fsdp": f + 1 - 2 * core}, device_id_type=mesh_id)

    own_rows = gathered.at[pl.ds(pl.multiple_of(f * here, here), here)]
    loads = [
        pltpu.make_async_copy(src, dst, load_sems.at[i])
        for i, (src, dst) in enumerate((
            (acts, acts_v), (proj_in, pin_v), (out_grads, outg_v), (proj_out, pout_v),
            (queries, own_rows), (store, score_rows.at[pl.ds(0, stored)])))
    ]
    for load in loads:
        load.start()

    barrier = pltpu.get_barrier_semaphore()

    def greet_plane(d, _):
        pl.semaphore_signal(barrier, inc=1, device_id=in_plane(d), device_id_type=mesh_id)
        return 0

    def greet_column(d, _):
        pl.semaphore_signal(barrier, inc=1, device_id=in_column(d), device_id_type=mesh_id)
        return 0

    lax.fori_loop(1, n_fsdp, greet_plane, 0)
    lax.fori_loop(1, n_grp, greet_column, 0)
    pl.semaphore_wait(barrier, n_fsdp - 1 + n_grp - 1)

    for p in range(min(early, cut)):
        for d in range(1, half):
            shard_copy(d, p).start()
    for load in loads[:5]:
        load.wait()
    for p in range(cut):
        pass_copy(0, p).start()

    tokens = lax.broadcasted_iota(jnp.int32, (length, 2 * rank), 0)
    lanes = lax.broadcasted_iota(jnp.int32, (rank, 2 * rank), 1)
    rows = lax.broadcasted_iota(jnp.int32, (rank, 2 * rank), 0)
    total = jnp.zeros((2 * rank, 2 * rank), F32)
    count = 0
    per_doc = []
    for doc in range(n_docs):
        in_proj = lax.dot_general(acts_v[doc], pin_v[...], NT, preferred_element_type=F32)
        out_proj = lax.dot_general(outg_v[doc], pout_v[...], NT, preferred_element_type=F32)
        both = jnp.concatenate([in_proj, out_proj], axis=1)
        size = lengths[doc]
        both = jnp.where(tokens < size, both, 0.0)
        gram = lax.dot_general(both, both, TN, precision=HIGHEST, preferred_element_type=F32)
        total = total + gram
        count = count + jnp.minimum(size, length)
        per_doc.append(gram[rank:, :rank] / size.astype(F32))
    packed = jnp.where(lanes < rank, total[:rank, :], total[rank:, :])
    counts = jnp.zeros((8, 2 * rank), F32) + count.astype(F32)
    for i in range(n_fsdp):
        piece = packed[i * share : (i + 1) * share, :]
        if share < 8:
            piece = jnp.concatenate([piece, jnp.zeros((8 - share, 2 * rank), F32)], axis=0)
        pieces[i, : piece.shape[0], :] = piece
        pieces[i, piece.shape[0] :, :] = counts

    def scatter_copy(d):
        return pltpu.make_async_remote_copy(
            src_ref=pieces.at[lax.rem(f + d, n_fsdp)], dst_ref=plane_slots.at[f],
            send_sem=ps.at[d], recv_sem=pr.at[d], device_id=in_plane(d), device_id_type=mesh_id)

    def column_copy(d):
        return pltpu.make_async_remote_copy(
            src_ref=column_slots.at[g], dst_ref=column_slots.at[g],
            send_sem=cs.at[d], recv_sem=cr.at[d], device_id=in_column(d), device_id_type=mesh_id)

    def total_copy(d):
        return pltpu.make_async_remote_copy(
            src_ref=totals.at[f], dst_ref=totals.at[f],
            send_sem=ts.at[d], recv_sem=tr.at[d], device_id=in_plane(d), device_id_type=mesh_id)

    for d in range(1, n_fsdp):
        scatter_copy(d).start()
    plane_slots[f] = pieces[f]
    flat = [
        jnp.concatenate([grad[a : a + 1, :] for a in range(rank)], axis=1) for grad in per_doc
    ]
    fresh = jnp.concatenate(
        flat + [jnp.zeros((score_rows.shape[0] - stored - n_docs, width), F32)], axis=0).astype(BF16)
    score_rows[stored:, :] = fresh
    new_grads[...] = fresh[:n_docs]
    for d in range(1, n_fsdp):
        scatter_copy(d).wait()
    summed = plane_slots[0]
    for i in range(1, n_fsdp):
        summed = summed + plane_slots[i]
    column_slots[g] = summed
    for d in range(1, n_grp):
        column_copy(d).start()
    for p in range(min(early, cut), min(2 * early, cut)):
        for d in range(1, half):
            shard_copy(d, p).start()
    for d in range(1, n_grp):
        column_copy(d).wait()
    summed = column_slots[0]
    for i in range(1, n_grp):
        summed = summed + column_slots[i]
    totals[f] = summed
    for d in range(1, n_fsdp):
        total_copy(d).start()
    for d in range(1, half):
        for p in range(min(2 * early, cut), cut):
            shard_copy(d, p).start()
    for d in range(1, n_fsdp):
        total_copy(d).wait()

    covariance = jnp.concatenate([totals[i, :share, :] for i in range(n_fsdp)], axis=0)
    covariance = covariance / summed[summed.shape[0] - 1 :, :]
    diagonal = (rows == lanes) | (rows + rank == lanes)
    on_diagonal = jnp.where(diagonal, covariance, 0.0)
    in_trace = jnp.sum(jnp.where(lanes < rank, on_diagonal, 0.0))
    out_trace = jnp.sum(jnp.where(lanes < rank, 0.0, on_diagonal))
    ridge = jnp.where(lanes < rank, 0.1 * in_trace / rank, 0.1 * out_trace / rank)
    both = invert_pair(covariance + jnp.where(diagonal, ridge, 0.0), rank)

    block = 4 * rank
    wide = jnp.concatenate([both[:, :rank]] * 4, axis=1)
    tiled = jnp.concatenate([wide] * 4, axis=0)
    r = lax.broadcasted_iota(jnp.int32, (block, block), 0) // rank
    c = lax.broadcasted_iota(jnp.int32, (block, block), 1) // rank
    in_parts = split3(jnp.where(r == c, tiled, 0.0))
    oh, om, ol = split3(both[:, rank:])
    left = jnp.concatenate([oh, oh, om, om, oh, ol], axis=1)

    load = loads[5]
    load.wait()
    unit_chips = UNIT // (2 * here)
    n_units = half // unit_chips

    def one_unit(e, _):
        unit = lax.rem(chip // unit_chips + n_units - e, n_units)
        for i in range(unit_chips):
            d = lax.rem(chip - (unit * unit_chips + i) + half, half)

            @pl.when(d != 0)
            def _():
                for p in range(cut):
                    shard_copy(d, p).wait()
                    pass_copy(d, p).start()

        for i in range(unit_chips):
            d = lax.rem(chip - (unit * unit_chips + i) + half, half)
            for p in range(cut):
                pass_copy(d, p).wait()
        here_rows = pl.ds(pl.multiple_of(unit * UNIT, UNIT), UNIT)
        for i in range(width // block):
            chunk = gathered[here_rows, i * block : (i + 1) * block]
            part = lax.dot_general(in_parts[0], chunk, NT, preferred_element_type=F32)
            part = part + lax.dot_general(in_parts[1], chunk, NT, preferred_element_type=F32)
            part = part + lax.dot_general(in_parts[2], chunk, NT, preferred_element_type=F32)
            for a in range(4):
                start = (4 * i + a) * pitch
                work[start : start + rank, :] = part[a * rank : (a + 1) * rank, :]
        for b in range(0, rank, 4):
            wheres = [pl.ds(b + j, rank, stride=pitch) for j in range(4)]
            half_done = jnp.concatenate([work[w, :] for w in wheres], axis=1)
            xh, xm, xl = split3(half_done)
            right = jnp.concatenate([xh, xm, xh, xm, xl, xh], axis=0)
            done = jnp.dot(left, right, preferred_element_type=F32)
            for j in range(4):
                work[wheres[j], :] = done[:, j * UNIT : (j + 1) * UNIT]
        prepared = jnp.concatenate(
            [work[a * pitch : a * pitch + rank, :].astype(BF16) for a in range(rank)], axis=0)
        scores = jnp.dot(score_rows[...], prepared, preferred_element_type=F32).astype(BF16)
        store_out[:, here_rows] = scores[:stored]
        new_out[:, here_rows] = scores[stored : stored + n_docs]
        return 0

    lax.fori_loop(0, n_units, one_unit, 0)


PIECE = 16
UNIT = 128


def influence(n_grp, n_fsdp, early, doc_lengths, acts, out_grads, proj_in, proj_out, queries, store):
    n_docs = acts.shape[0]
    rank = proj_in.shape[0]
    here, width = queries.shape
    stored = store.shape[0]
    n_queries = n_fsdp * here
    dma = pltpu.SemaphoreType.DMA
    slot = (-(-(rank // n_fsdp) // 8) * 8 + 8, 2 * rank)
    score_rows = -(-(stored + n_docs) // 16) * 16
    copies = dma((n_fsdp // 2 * (here // PIECE),))
    return pl.pallas_call(
        functools.partial(influence_kernel, n_grp, n_fsdp, early),
        out_shape=(
            jax.ShapeDtypeStruct((n_docs, width), BF16),
            jax.ShapeDtypeStruct((stored, n_queries), BF16),
            jax.ShapeDtypeStruct((n_docs, n_queries), BF16),
        ),
        in_specs=[pl.BlockSpec(memory_space=pltpu.SMEM)] + [pl.BlockSpec(memory_space=ANY)] * 6,
        out_specs=tuple([pl.BlockSpec(memory_space=VMEM)] * 3),
        scratch_shapes=[
            VMEM(acts.shape, BF16), VMEM(out_grads.shape, BF16),
            VMEM(proj_in.shape, BF16), VMEM(proj_out.shape, BF16),
            VMEM((n_queries, width), BF16), VMEM((score_rows, width), BF16),
            VMEM((rank * (rank + 8), UNIT), F32),
            VMEM((n_fsdp,) + slot, F32), VMEM((n_fsdp,) + slot, F32),
            VMEM((n_grp,) + slot, F32), VMEM((n_fsdp,) + slot, F32),
            dma((6,)), copies, copies, copies, copies,
            dma((n_fsdp,)), dma((n_fsdp,)), dma((n_grp,)), dma((n_grp,)), dma((n_fsdp,)), dma((n_fsdp,)),
        ],
        compiler_params=pltpu.CompilerParams(
            collective_id=0, has_side_effects=True, vmem_limit_bytes=60 * 2**20),
    )(doc_lengths, acts, out_grads, proj_in, proj_out, queries, store)


def solution(mesh):
    n_grp, n_fsdp = mesh.shape["grp"], mesh.shape["fsdp"]

    def shards(acts, out_grads, doc_lengths, proj_in, proj_out, store_grads, queries):
        return influence(
            n_grp, n_fsdp, 1, doc_lengths, acts, out_grads, proj_in, proj_out, queries, store_grads)

    rows = P(("grp", "fsdp"), None)
    placed = (
        P(("grp", "fsdp"), None, None),
        P(("grp", "fsdp"), None, None),
        P(("grp", "fsdp")),
        P(),
        P(),
        rows,
        P("fsdp", None),
    )
    return jax.shard_map(
        shards, mesh=mesh, in_specs=placed, out_specs=(rows, rows, rows), check_vma=False)
```
